512 devices in a mesh: ctx: 16 (over x, y), ep: 32 (over z, core).
Axes of the slice: x: 4, y: 4, z: 16, core: 2. Of those that a mesh axis runs over, the one named last changes fastest.
Arguments:
- queries: bfloat16 [32, 2048, 4096], P('ep', 'ctx'), may hold values from -7 to 7
- keys: bfloat16 [32, 2048, 256], P('ep', 'ctx'), may hold values from -4.5 to 4.5
- values: bfloat16 [32, 2048, 256], P('ep', 'ctx'), may hold values from -5 to 5
- hidden: bfloat16 [32, 2048, 2048], P('ep', 'ctx'), may hold values from -130 to 130
- expert_ids: int32 [32, 2048, 2], P('ep', 'ctx'), may hold values from 0 to 31, all different within a row; in each aligned block of 128 rows (0 to 127, 128 to 255, ..., all dimensions but the last counted through in order) at most 12 rows name the same one
- gate_probs: float32 [32, 2048, 2], P('ep', 'ctx'), may hold values from 0.2 to 1
- norm_gain: float32 [2048], replicated, may hold values from 0.1 to 1.9
- w_gate: bfloat16 [32, 768, 2048], P('ep', 'ctx'), may hold values from -0.125 to 0.125
- w_up: bfloat16 [32, 768, 2048], P('ep', 'ctx'), may hold values from -0.125 to 0.125
- w_down: bfloat16 [32, 768, 2048], P('ep', 'ctx'), may hold values from -0.21875 to 0.21875
Outputs:
- attended: bfloat16 [32, 2048, 4096], P('ep', 'ctx')
- expert_mix: bfloat16 [32, 2048, 2048], P('ep', 'ctx')
The draws below stay inside these ranges and needn't reach their ends.
Inputs may be any that keep to these rules, and one draw needn't show every extreme that they name: `expert_ids`: the 2 experts of one token differ. Among the 128 tokens of one device no expert is named more than 12 times.
All inputs are finite; a program needn't handle non-finite values.
Results may differ from the reference program's by a relative error of at most 0.0071.
Values may be sent and summed in bfloat16 or wider, within the bound.
No kernel may reach another device: no remote copies, remote signals or barrier semaphores. Data moves between devices by JAX's collectives and lax.ppermute only.
A program may use at most 128 MiB of HBM per device.

```python
import math
import jax
import jax.numpy as jnp
import numpy as np
from jax import lax

D = 2048
HQ = 32
KVH = 2
DH = 128
H = 768
ROUTES = 2
TOK_DEV = 128
SEQ = 2048
BATCH = 32
EXPERTS = 32
CAP = 12
N_CTX = 16
N_EP = 32


def draw_queries(key, part):
    shape = (BATCH, SEQ, HQ * DH)
    base = jnp.clip(jax.random.normal(jax.random.fold_in(key, 21), shape, jnp.float32), -4.5, 4.5)
    return base.astype(jnp.bfloat16)


def draw_keys(key, part):
    shape = (BATCH, SEQ, KVH * DH)
    base = jnp.clip(jax.random.normal(jax.random.fold_in(key, 22), shape, jnp.float32), -4.5, 4.5)
    return base.astype(jnp.bfloat16)


def draw_hidden(key, part):
    shape = (BATCH, SEQ, D)
    column_scale = jnp.exp(jax.random.uniform(jax.random.fold_in(key, 31), (1, 1, D), jnp.float32, 0.0, math.log(10.0)))
    base = jnp.clip(jax.random.normal(jax.random.fold_in(key, 33), shape, jnp.float32), -4.0, 4.0)
    row_scale = jnp.exp(jax.random.uniform(jax.random.fold_in(key, 34), (BATCH, SEQ, 1), jnp.float32, 0.0, math.log(10.0)))
    return (0.3 * base * row_scale * column_scale).astype(jnp.bfloat16)


def shard_levels(stream_key, dims, cuts, least, largest):
    loudness, own = 1.0, jax.random.fold_in(stream_key, 6)
    for dim, blocks in cuts:
        heights = jnp.exp(jax.random.uniform(jax.random.fold_in(own, dim), (blocks,), jnp.float32, least / len(cuts), largest / len(cuts)))
        loudness = loudness * jnp.repeat(heights, dims[dim] // blocks).reshape([-1 if axis == dim else 1 for axis in range(len(dims))])
    return loudness


def assign_block(stream_key, own, number, rows, count, top, limit, slope):
    sequence = jax.random.permutation(stream_key, count)
    packed, ordinary = shares(count, rows * top, limit, slope, True), shares(count, rows * top, limit, slope, False)
    places = jnp.arange(count)

    def named(tallies, offset_by):
        used = int((tallies > 0).sum())
        fixed = max(1, used // 4)
        shifted = fixed + (places - fixed + offset_by * (used - fixed)) % max(1, count - fixed)
        return jnp.zeros((count,), jnp.int32).at[sequence[jnp.where(places < fixed, places, shifted)]].set(jnp.asarray(tallies, jnp.int32))

    tallies = jnp.where(number % 4 == 0, named(packed, number // 4), named(ordinary, number - number // 4 - 1))
    mixed = jax.random.permutation(jax.random.fold_in(own, 3), count)
    giver, taker = mixed[0:count // 2 * 2:2], mixed[1:count // 2 * 2:2]
    margin = jnp.minimum(tallies[giver] - 1, limit - tallies[taker]) // 2
    margin = jnp.where((giver == sequence[0]) | (taker == sequence[0]) | (tallies[taker] == 0), 0, jnp.maximum(margin, 0))
    shifted = jax.random.randint(jax.random.fold_in(own, 4), (count // 2,), 0, 1 << 20) % (margin + 1)
    tallies = tallies.at[giver].add(-shifted).at[taker].add(shifted)
    items = jnp.searchsorted(jnp.cumsum(tallies), jnp.arange(rows * top), side="right").astype(jnp.int32)
    table = items.reshape(top, rows).T
    table = table[jax.random.permutation(jax.random.fold_in(own, 1), rows)]
    offset_by = jax.random.randint(jax.random.fold_in(own, 2), (rows, 1), 0, top)
    return jnp.take_along_axis(table, (jnp.arange(top)[None, :] + offset_by) % top, axis=1)


def shares(count, total, limit, skew, full):
    weights = [(1 << 20) // math.isqrt(rank ** skew) + 1 for rank in range(1, count + 1)]
    largest = limit if full else min(limit, max(-(-total // count), total * weights[0] // sum(weights)))
    least = 1 if total - largest >= count - 1 else 0
    holding, spare = [largest] + [least] * (count - 1), total - largest - least * (count - 1)
    while spare > 0:
        candidates = [i for i in range(1, count) if holding[i] < largest] or [i for i in range(1, count) if holding[i] < limit]
        whole, left = sum([weights[i] for i in candidates]), spare
        for i in candidates:
            extra = min(limit - holding[i], max(1, left * weights[i] // whole), spare)
            holding[i] = holding[i] + extra
            spare = spare - extra
    return np.array(holding)


def scatter_about(key, extent, width, most, split=(), held_as=jnp.bfloat16):
    loudness = shard_levels(key, extent, split, -0.22, 0.18) if split else 1.0
    drawn = jax.random.normal(key, extent, jnp.float32) * width * loudness
    return jnp.minimum(jnp.maximum(drawn, -most), most).astype(held_as)


def setup_inputs(seed: int = 0) -> dict:
    key_list = jax.random.split(jax.random.key(seed), 11)
    queries = draw_queries(jax.random.fold_in(key_list[10], 71), 0)
    keys = draw_keys(jax.random.fold_in(key_list[10], 71), 0)
    values = scatter_about(key_list[2], (BATCH, SEQ, KVH * DH), 1.0, 5.0, ((0, 32), (1, 16)))
    hidden = draw_hidden(jax.random.fold_in(key_list[10], 71), 0)
    expert_ids_keys = jax.random.split(jax.random.fold_in(key_list[4], 1), BATCH * SEQ // TOK_DEV)
    expert_ids_turns = jax.random.permutation(jax.random.fold_in(key_list[4], 3), BATCH * SEQ // TOK_DEV)
    expert_ids = jax.vmap(lambda own, number: assign_block(jax.random.fold_in(key_list[4], 2), own, number, TOK_DEV, EXPERTS, ROUTES, CAP, 2))(expert_ids_keys, expert_ids_turns).reshape((BATCH, SEQ, ROUTES))
    gate_probs = jnp.clip(0.2 + 0.8 * jax.random.uniform(key_list[5], (BATCH, SEQ, ROUTES), jnp.float32) ** shard_levels(key_list[5], (BATCH, SEQ, ROUTES), ((0, 32), (1, 16)), -0.2, 0.2), 0.2, 1.0)
    norm_gain = jnp.clip(1.0 + 0.18 * jax.random.normal(key_list[6], (D,), jnp.float32), 0.1, 1.9)
    w_gate = scatter_about(key_list[7], (EXPERTS, H, D), D ** -0.5, 0.125, ((0, 32), (1, 16)))
    w_up = scatter_about(key_list[8], (EXPERTS, H, D), D ** -0.5, 0.125, ((0, 32), (1, 16)))
    w_down = scatter_about(key_list[9], (EXPERTS, H, D), H ** -0.5, 0.21875, ((0, 32), (1, 16)))
    return dict(queries=queries, keys=keys, values=values, hidden=hidden, expert_ids=expert_ids, gate_probs=gate_probs, norm_gain=norm_gain, w_gate=w_gate, w_up=w_up, w_down=w_down)


def attend_sequence(operands):
    query_seq, key_seq, value_seq = operands
    block_count = SEQ // TOK_DEV
    score_factor = 1.0 / math.sqrt(DH)
    query_blocks = query_seq.reshape(block_count, TOK_DEV, KVH, HQ // KVH, DH).astype(jnp.float32)
    key_heads = key_seq.reshape(SEQ, KVH, DH).astype(jnp.float32)
    value_heads = value_seq.reshape(SEQ, KVH, DH).astype(jnp.float32)
    key_pos = jnp.arange(SEQ, dtype=jnp.int32)

    def attend_block(block_item):
        query_block, block_index = block_item
        scores = jnp.einsum('rgjd,ngd->gjrn', query_block, key_heads) * score_factor
        query_pos = block_index * TOK_DEV + jnp.arange(TOK_DEV, dtype=jnp.int32)
        visible = key_pos[None, :] <= query_pos[:, None]
        scores = jnp.where(visible, scores, -jnp.inf)
        maxima = lax.optimization_barrier(jnp.max(scores, axis=-1, keepdims=True))
        exponent = jnp.exp(scores - maxima)
        totals = lax.optimization_barrier(jnp.sum(exponent, axis=-1))
        weights = lax.optimization_barrier(exponent.astype(jnp.bfloat16)).astype(jnp.float32)
        weighted = jnp.einsum('gjrn,ngd->rgjd', weights, value_heads)
        result = weighted / jnp.transpose(totals, (2, 0, 1))[..., None]
        return result.reshape(TOK_DEV, HQ * DH).astype(jnp.bfloat16)
    blocks = lax.map(attend_block, (query_blocks, jnp.arange(block_count, dtype=jnp.int32)))
    return blocks.reshape(SEQ, HQ * DH)

def reference(queries, keys, values, hidden, expert_ids, gate_probs, norm_gain, w_gate, w_up, w_down):
    attended = lax.map(attend_sequence, (queries, keys, values))
    token_count = BATCH * SEQ
    tokens = hidden.reshape(token_count, D).astype(jnp.float32)
    mean_square = lax.optimization_barrier(jnp.mean(tokens * tokens, axis=-1, keepdims=True))
    normed = (tokens * lax.rsqrt(mean_square + 1e-06) * norm_gain).astype(jnp.bfloat16)
    route_ids = expert_ids.reshape(token_count, ROUTES)
    route_weight = gate_probs.reshape(token_count, ROUTES)
    row_limit = N_CTX * N_EP * CAP

    def add_expert(expert, mixture):
        chosen = route_ids == expert
        token_weight = lax.optimization_barrier(jnp.sum(jnp.where(chosen, route_weight, 0.0), axis=-1))
        row_index = jnp.nonzero(jnp.any(chosen, axis=-1), size=row_limit, fill_value=token_count)[0].astype(jnp.int32)
        gathered = jnp.take(normed, row_index, axis=0, mode='fill', fill_value=0)
        gate_pre = jnp.dot(gathered, w_gate[expert].T, preferred_element_type=jnp.float32)
        up_pre = jnp.dot(gathered, w_up[expert].T, preferred_element_type=jnp.float32)
        activated = (jax.nn.silu(gate_pre) * up_pre).astype(jnp.bfloat16)
        expert_out = jnp.dot(activated, w_down[expert], preferred_element_type=jnp.float32).astype(jnp.bfloat16)
        weight_rows = jnp.take(token_weight, row_index, axis=0, mode='fill', fill_value=0)
        contribution = weight_rows[:, None] * expert_out.astype(jnp.float32)
        return mixture.at[row_index].add(contribution, mode='drop')
    mixture = lax.fori_loop(0, EXPERTS, add_expert, jnp.zeros((token_count, D), jnp.float32))
    expert_mix = mixture.astype(jnp.bfloat16).reshape(BATCH, SEQ, D)
    return (attended, expert_mix)
```

```python
import functools
import math

import jax
import jax.numpy as jnp
from jax import lax
from jax.experimental import pallas as pl
from jax.experimental.pallas import tpu as pltpu
from jax.sharding import PartitionSpec as P

HQ = 32
KVH = 2
DH = 128
CAP = 12
WHOLE = 8
CHUNK = 512
PAIRS = 4
VMEM = 40 << 20
BF16 = jnp.bfloat16
F32 = jnp.float32


def dot(a, b):
    return jnp.dot(a, b, preferred_element_type=F32)


def dot_nt(a, b):
    return lax.dot_general(a, b, (((1,), (1,)), ((), ())), preferred_element_type=F32)


def dispatch_kernel(hidden_ref, ids_ref, gain_ref, out_ref, place_ref):
    rows, width = hidden_ref.shape
    half = width // 2
    experts = out_ref.shape[0] // WHOLE
    tokens = hidden_ref[...].astype(F32)
    mean_square = jnp.mean(tokens * tokens, axis=-1, keepdims=True)
    normed = (tokens * lax.rsqrt(mean_square + 1e-06) * gain_ref[...]).astype(BF16)

    ids = ids_ref[...]
    first, second = ids[0:1, :], ids[1:2, :]
    expert_iota = lax.broadcasted_iota(jnp.int32, (experts, rows), 0)
    hot = [(expert_iota == ids_row).astype(F32) for ids_row in (first, second)]
    earlier = (
        lax.broadcasted_iota(jnp.int32, (rows, rows), 0)
        < lax.broadcasted_iota(jnp.int32, (rows, rows), 1)
    ).astype(BF16)
    before = [dot(h.astype(BF16), earlier) for h in hot]
    before[1] = before[1] + jnp.sum(hot[0], axis=1, keepdims=True)
    slots = [
        jnp.sum(h * b, axis=0, keepdims=True).astype(jnp.int32) for h, b in zip(hot, before)
    ]
    whole = [
        jnp.where(s < WHOLE, e * WHOLE + s, -1) for e, s in zip((first, second), slots)
    ]
    halves = [
        jnp.where(s < WHOLE, -2, e * WHOLE + 2 * (s - WHOLE))
        for e, s in zip((first, second), slots)
    ]
    slot_iota = lax.broadcasted_iota(jnp.int32, (experts * WHOLE, rows), 0)

    def onehot(targets):
        return ((slot_iota == targets[0]) | (slot_iota == targets[1])).astype(F32).astype(BF16)

    out_ref[:, :width] = dot(onehot(whole), normed).astype(BF16)
    out_ref[:, width:] = (
        dot(onehot(halves), normed[:, :half])
        + dot(onehot([h + 1 for h in halves]), normed[:, half:])
    ).astype(BF16)
    place_ref[...] = jnp.concatenate(whole + halves + whole + halves, axis=0)


def dispatch(hidden, ids, gain, experts):
    rows, width = hidden.shape
    return pl.pallas_call(
        dispatch_kernel,
        out_shape=(
            jax.ShapeDtypeStruct((experts * WHOLE, width + width // 2), BF16),
            jax.ShapeDtypeStruct((8, rows), jnp.int32),
        ),
        compiler_params=pltpu.CompilerParams(vmem_limit_bytes=VMEM),
        name="dispatch",
    )(hidden, ids, gain)


def expert_kernel(rows_ref, weights_ref, out_ref, x_ref, y_ref, act_ref, w_ref, sems):
    count = rows_ref.shape[0]
    width = x_ref.shape[1]
    half = width // 2
    hidden = w_ref.shape[1]
    steps = 3
    span = hidden // steps
    copies = {}
    for step in range(steps):
        for part in range(2):
            copies[part, step] = pltpu.make_async_copy(
                weights_ref.at[pl.ds(step * span, span), pl.ds(part * width, width)],
                w_ref.at[part, pl.ds(step * span, span), :],
                sems.at[2 * step + part],
            )
    copies[2, 0] = pltpu.make_async_copy(
        weights_ref.at[:, pl.ds(2 * width, width)], w_ref.at[2], sems.at[2 * steps]
    )
    for copy in copies.values():
        copy.start()

    extra = count // 2
    pick_row = lax.broadcasted_iota(jnp.int32, (extra, count), 0)
    pick_col = lax.broadcasted_iota(jnp.int32, (extra, count), 1)
    x_ref[pl.ds(0, count), :] = rows_ref[:, :width]
    tail = rows_ref[:, width:]
    for part in range(2):
        pick = (pick_col == 2 * pick_row + part).astype(F32).astype(BF16)
        x_ref[pl.ds(count, extra), pl.ds(part * half, half)] = dot(pick, tail).astype(BF16)

    for step in range(steps):
        for part in range(2):
            copies[part, step].wait()
        x = x_ref[...]
        gate_pre = dot_nt(x, w_ref[0, pl.ds(step * span, span), :])
        up_pre = dot_nt(x, w_ref[1, pl.ds(step * span, span), :])
        act_ref[:, pl.ds(step * span, span)] = (
            gate_pre / (1.0 + jnp.exp(-gate_pre)) * up_pre
        ).astype(BF16)
    copies[2, 0].wait()
    act = act_ref[...]
    piece = width // 4
    for step in range(4):
        lanes = pl.ds(step * piece, piece)
        y = dot(act, w_ref[2, :, lanes]).astype(BF16)
        out_ref[:, lanes] = y[:count]
        y_ref[:, lanes] = y[count:]
    put_row = lax.broadcasted_iota(jnp.int32, (count, extra), 0)
    put_col = lax.broadcasted_iota(jnp.int32, (count, extra), 1)
    total = 0.0
    for part in range(2):
        put = (put_row == 2 * put_col + part).astype(F32).astype(BF16)
        total = total + dot(put, y_ref[:, pl.ds(part * half, half)])
    out_ref[:, width:] = total.astype(BF16)


def expert(rows, weights):
    count = rows.shape[0]
    hidden, width = weights.shape[0], weights.shape[1] // 3
    total = count // WHOLE * CAP
    return pl.pallas_call(
        expert_kernel,
        out_shape=jax.ShapeDtypeStruct(rows.shape, BF16),
        in_specs=[
            pl.BlockSpec(memory_space=pltpu.VMEM),
            pl.BlockSpec(memory_space=pltpu.HBM),
        ],
        out_specs=pl.BlockSpec(memory_space=pltpu.VMEM),
        scratch_shapes=[
            pltpu.VMEM((total, width), BF16),
            pltpu.VMEM((total - count, width), BF16),
            pltpu.VMEM((total, hidden), BF16),
            pltpu.VMEM((3, hidden, width), BF16),
            pltpu.SemaphoreType.DMA((7,)),
        ],
        compiler_params=pltpu.CompilerParams(vmem_limit_bytes=56 << 20),
        cost_estimate=pl.CostEstimate(
            flops=6 * total * hidden * width,
            bytes_accessed=2 * weights.size + 4 * rows.size,
            transcendentals=total * hidden,
        ),
        name="expert",
    )(rows, weights)


def combine_kernel(returned_ref, place_ref, prob_ref, out_ref):
    count = returned_ref.shape[0]
    rows, width = out_ref.shape
    half = width // 2
    place = place_ref[...].astype(F32).T.astype(jnp.int32)
    prob = prob_ref[...].T
    slot_iota = lax.broadcasted_iota(jnp.int32, (rows, count), 1)

    def onehot(column):
        return (slot_iota == column).astype(F32).astype(BF16)

    whole = [onehot(place[:, route : route + 1]) for route in range(2)]
    for part in range(2):
        lanes = pl.ds(part * half, half)
        mixture = 0.0
        for route in range(2):
            picked = dot(whole[route], returned_ref[:, lanes]) + dot(
                onehot(place[:, 2 + route : 3 + route] + part), returned_ref[:, width:]
            )
            mixture = mixture + prob[:, route : route + 1] * picked
        out_ref[:, lanes] = mixture.astype(BF16)


def combine(returned, place, prob):
    rows, width = place.shape[1], returned.shape[1] // 3 * 2
    return pl.pallas_call(
        combine_kernel,
        out_shape=jax.ShapeDtypeStruct((rows, width), BF16),
        compiler_params=pltpu.CompilerParams(vmem_limit_bytes=VMEM),
        name="combine",
    )(returned, place, prob)


def attention_kernel(block_ref, query_ref, key_ref, value_ref, out_ref, vt_ref, *score_refs):
    block = block_ref[0]
    rows = query_ref.shape[0]
    seq = key_ref.shape[0]
    width = 2 * rows
    factor = math.log2(math.e) / math.sqrt(DH)

    @pl.when(pl.program_id(1) == 0)
    def _():
        vt_ref[...] = value_ref[...].T

    row_less_key = (
        block * rows
        + lax.rem(lax.broadcasted_iota(jnp.int32, (CHUNK, width), 1), jnp.int32(rows))
        - lax.broadcasted_iota(jnp.int32, (CHUNK, width), 0)
    )

    def scores(pair, chunks):
        first = query_ref[:, 2 * pair * DH : (2 * pair + 1) * DH]
        second = query_ref[:, (2 * pair + 1) * DH : (2 * pair + 2) * DH]
        query_t = jnp.concatenate([first.T, second.T], axis=1)
        tops = []
        for chunk in range(chunks):
            at = slice(chunk * CHUNK, (chunk + 1) * CHUNK)
            raw = dot(key_ref[at, :], query_t)
            if chunk == chunks - 1:
                raw = jnp.where(row_less_key >= chunk * CHUNK, raw, -jnp.inf)
            score_refs[pair][at, :] = raw
            tops.append(jnp.max(raw, axis=0, keepdims=True))
        return functools.reduce(jnp.maximum, tops)

    def weigh(pair, chunks, top):
        total, weighted = 0.0, 0.0
        for chunk in range(chunks):
            at = slice(chunk * CHUNK, (chunk + 1) * CHUNK)
            prob = jnp.exp2((score_refs[pair][at, :] - top) * factor)
            weighted = weighted + dot(vt_ref[:, at], prob.astype(BF16))
            total = total + jnp.sum(prob, axis=0, keepdims=True)
        result = weighted / total
        for head in range(2):
            out_ref[:, (2 * pair + head) * DH : (2 * pair + head + 1) * DH] = (
                result[:, head * rows : (head + 1) * rows].T.astype(BF16)
            )

    for chunks in range(1, seq // CHUNK + 1):

        @pl.when(block * rows // CHUNK + 1 == chunks)
        def _():
            top = scores(0, chunks)
            for pair in range(1, PAIRS):
                next_top = scores(pair, chunks)
                weigh(pair - 1, chunks, top)
                top = next_top
            weigh(PAIRS - 1, chunks, top)


def attention(block, queries, keys_values):
    rows = queries.shape[0]
    seq = keys_values.shape[0]
    steps = HQ // KVH // 2 // PAIRS
    span = 2 * PAIRS * DH
    return pl.pallas_call(
        attention_kernel,
        out_shape=jax.ShapeDtypeStruct(queries.shape, BF16),
        grid_spec=pltpu.PrefetchScalarGridSpec(
            num_scalar_prefetch=1,
            grid=(KVH, steps),
            in_specs=[
                pl.BlockSpec((rows, span), lambda g, p, b: (0, g * steps + p)),
                pl.BlockSpec((seq, DH), lambda g, p, b: (0, g)),
                pl.BlockSpec((seq, DH), lambda g, p, b: (0, KVH + g)),
            ],
            out_specs=pl.BlockSpec((rows, span), lambda g, p, b: (0, g * steps + p)),
            scratch_shapes=[pltpu.VMEM((DH, seq), BF16)]
            + [pltpu.VMEM((seq, 2 * rows), F32)] * PAIRS,
        ),
        compiler_params=pltpu.CompilerParams(
            dimension_semantics=("arbitrary", "arbitrary"), vmem_limit_bytes=VMEM
        ),
        cost_estimate=pl.CostEstimate(
            flops=4 * rows * seq * HQ * DH,
            bytes_accessed=4 * queries.size + 2 * keys_values.size,
            transcendentals=rows * seq * HQ,
        ),
        name="attention",
    )(block, queries, keys_values, keys_values)


def per_device(
    queries, keys, values, hidden, expert_ids, gate_probs, norm_gain, w_gate, w_up, w_down
):
    experts = lax.axis_size("ep")
    width = hidden.shape[2]
    shards = jnp.concatenate([w_gate[0], w_up[0], w_down[0]], axis=1)
    weights = lax.all_gather(shards, "ctx", axis=0, tiled=True)

    outgoing, place = dispatch(hidden[0], expert_ids[0].T, norm_gain[None], experts)
    keys_values = jnp.concatenate([keys[0], values[0]], axis=1)
    outgoing, keys_values = lax.optimization_barrier((outgoing, keys_values))
    keys_values = lax.all_gather(keys_values, "ctx", axis=0, tiled=True)

    def exchange(rows):
        moved = lax.all_to_all(
            rows.reshape(experts, WHOLE, rows.shape[1]), "ep", split_axis=0, concat_axis=0, tiled=True
        )
        return moved.reshape(rows.shape)

    produced = expert(exchange(outgoing), weights)
    produced, queries = lax.optimization_barrier((produced, queries))
    returned = exchange(produced)
    block = lax.axis_index("ctx").astype(jnp.int32)[None]
    attended = attention(block, queries[0], keys_values)
    mixed = combine(returned, place, gate_probs[0].T)
    return (attended[None], mixed[None])


def solution(mesh):
    split = P("ep", "ctx", None)
    return jax.shard_map(
        per_device,
        mesh=mesh,
        in_specs=(split,) * 6 + (P(),) + (split,) * 3,
        out_specs=(split, split),
        check_vma=False,
    )
```

```python
import functools
import math

import jax
import jax.numpy as jnp
from jax import lax
from jax.experimental import pallas as pl
from jax.experimental.pallas import tpu as pltpu
from jax.sharding import PartitionSpec as P

HQ = 32
KVH = 2
DH = 128
CAP = 12
WHOLE = 8
CHUNK = 512
RING = 4
HIDDEN_STEP = 256
PAIRS = 4
VMEM = 16 << 20
BF16 = jnp.bfloat16
F32 = jnp.float32


def dot(a, b):
    return jnp.dot(a, b, preferred_element_type=F32)


def dot_nt(a, b):
    return lax.dot_general(a, b, (((1,), (1,)), ((), ())), preferred_element_type=F32)


def dispatch_kernel(hidden_ref, ids_ref, gain_ref, out_ref, place_ref):
    rows, width = hidden_ref.shape
    half = width // 2
    experts = out_ref.shape[0] // WHOLE
    tokens = hidden_ref[...].astype(F32)
    mean_square = jnp.mean(tokens * tokens, axis=-1, keepdims=True)
    normed = (tokens * lax.rsqrt(mean_square + 1e-06) * gain_ref[...]).astype(BF16)

    ids = ids_ref[...]
    first, second = ids[0:1, :], ids[1:2, :]
    expert_iota = lax.broadcasted_iota(jnp.int32, (experts, rows), 0)
    hot = [(expert_iota == ids_row).astype(F32) for ids_row in (first, second)]
    earlier = (
        lax.broadcasted_iota(jnp.int32, (rows, rows), 0)
        < lax.broadcasted_iota(jnp.int32, (rows, rows), 1)
    ).astype(BF16)
    before = [dot(h.astype(BF16), earlier) for h in hot]
    before[1] = before[1] + jnp.sum(hot[0], axis=1, keepdims=True)
    slots = [
        jnp.sum(h * b, axis=0, keepdims=True).astype(jnp.int32) for h, b in zip(hot, before)
    ]
    whole = [
        jnp.where(s < WHOLE, e * WHOLE + s, -1) for e, s in zip((first, second), slots)
    ]
    halves = [
        jnp.where(s < WHOLE, -2, e * WHOLE + 2 * (s - WHOLE))
        for e, s in zip((first, second), slots)
    ]
    slot_iota = lax.broadcasted_iota(jnp.int32, (experts * WHOLE, rows), 0)

    def onehot(targets):
        return ((slot_iota == targets[0]) | (slot_iota == targets[1])).astype(F32).astype(BF16)

    out_ref[:, :width] = dot(onehot(whole), normed).astype(BF16)
    out_ref[:, width:] = (
        dot(onehot(halves), normed[:, :half])
        + dot(onehot([h + 1 for h in halves]), normed[:, half:])
    ).astype(BF16)
    place_ref[...] = jnp.concatenate(whole + halves + whole + halves, axis=0)


def dispatch(hidden, ids, gain, experts):
    rows, width = hidden.shape
    return pl.pallas_call(
        dispatch_kernel,
        out_shape=(
            jax.ShapeDtypeStruct((experts * WHOLE, width + width // 2), BF16),
            jax.ShapeDtypeStruct((8, rows), jnp.int32),
        ),
        compiler_params=pltpu.CompilerParams(vmem_limit_bytes=VMEM),
        name="dispatch",
    )(hidden, ids, gain)


def expert_kernel(rows_ref, *refs):
    *piece_refs, out_ref, x_ref, y_ref, act_ref, w_ref, sems = refs
    count = rows_ref.shape[0]
    width = x_ref.shape[1]
    half = width // 2
    hidden = act_ref.shape[1]
    copies, base = [], 0
    for index, ref in enumerate(piece_refs):
        place = w_ref.at[pl.ds(base, ref.shape[0]), :]
        copies.append((base, pltpu.make_async_copy(ref, place, sems.at[index])))
        base += ref.shape[0]
    for _, copy in copies:
        copy.start()

    extra = count // 2
    pick_row = lax.broadcasted_iota(jnp.int32, (extra, count), 0)
    pick_col = lax.broadcasted_iota(jnp.int32, (extra, count), 1)
    x_ref[pl.ds(0, count), :] = rows_ref[:, :width]
    tail = rows_ref[:, width:]
    for part in range(2):
        pick = (pick_col == 2 * pick_row + part).astype(F32).astype(BF16)
        x_ref[pl.ds(count, extra), pl.ds(part * half, half)] = dot(pick, tail).astype(BF16)

    for start in range(0, hidden, HIDDEN_STEP):
        stop = start + HIDDEN_STEP
        while copies and copies[0][0] < stop:
            copies.pop(0)[1].wait()
        x = x_ref[...]
        gate_pre = dot_nt(x, w_ref[start:stop, :width])
        up_pre = dot_nt(x, w_ref[start:stop, width : 2 * width])
        act_ref[:, start:stop] = (gate_pre / (1.0 + jnp.exp(-gate_pre)) * up_pre).astype(BF16)
    act = act_ref[...]
    piece = width // 4
    for step in range(4):
        lanes = slice(step * piece, (step + 1) * piece)
        y = dot(act, w_ref[:, 2 * width + lanes.start : 2 * width + lanes.stop]).astype(BF16)
        out_ref[:, lanes] = y[:count]
        y_ref[:, lanes] = y[count:]
    put_row = lax.broadcasted_iota(jnp.int32, (count, extra), 0)
    put_col = lax.broadcasted_iota(jnp.int32, (count, extra), 1)
    total = 0.0
    for part in range(2):
        put = (put_row == 2 * put_col + part).astype(F32).astype(BF16)
        total = total + dot(put, y_ref[:, pl.ds(part * half, half)])
    out_ref[:, width:] = total.astype(BF16)


def expert(rows, pieces):
    count = rows.shape[0]
    hidden, width = sum(p.shape[0] for p in pieces), pieces[0].shape[1] // 3
    total = count // WHOLE * CAP
    return pl.pallas_call(
        expert_kernel,
        out_shape=jax.ShapeDtypeStruct(rows.shape, BF16),
        in_specs=[pl.BlockSpec(memory_space=pltpu.VMEM)]
        + [pl.BlockSpec(memory_space=pl.ANY)] * len(pieces),
        out_specs=pl.BlockSpec(memory_space=pltpu.VMEM),
        scratch_shapes=[
            pltpu.VMEM((total, width), BF16),
            pltpu.VMEM((total - count, width), BF16),
            pltpu.VMEM((total, hidden), BF16),
            pltpu.VMEM((hidden, 3 * width), BF16),
            pltpu.SemaphoreType.DMA((len(pieces),)),
        ],
        compiler_params=pltpu.CompilerParams(vmem_limit_bytes=56 << 20),
        cost_estimate=pl.CostEstimate(
            flops=6 * total * hidden * width,
            bytes_accessed=6 * hidden * width + 4 * rows.size,
            transcendentals=total * hidden,
        ),
        name="expert",
    )(rows, *pieces)


def combine_kernel(returned_ref, place_ref, prob_ref, out_ref):
    count = returned_ref.shape[0]
    rows, width = out_ref.shape
    half = width // 2
    place = place_ref[...].astype(F32).T.astype(jnp.int32)
    prob = prob_ref[...].T
    slot_iota = lax.broadcasted_iota(jnp.int32, (rows, count), 1)

    def onehot(column):
        return (slot_iota == column).astype(F32).astype(BF16)

    whole = [onehot(place[:, route : route + 1]) for route in range(2)]
    for part in range(2):
        lanes = pl.ds(part * half, half)
        mixture = 0.0
        for route in range(2):
            picked = dot(whole[route], returned_ref[:, lanes]) + dot(
                onehot(place[:, 2 + route : 3 + route] + part), returned_ref[:, width:]
            )
            mixture = mixture + prob[:, route : route + 1] * picked
        out_ref[:, lanes] = mixture.astype(BF16)


def combine(returned, place, prob):
    rows, width = place.shape[1], returned.shape[1] // 3 * 2
    return pl.pallas_call(
        combine_kernel,
        out_shape=jax.ShapeDtypeStruct((rows, width), BF16),
        compiler_params=pltpu.CompilerParams(vmem_limit_bytes=VMEM),
        name="combine",
    )(returned, place, prob)


OFFSETS = (0, -1, 1, 2)
SOURCES = [(dx, dy) for dx in (0, -1, 1) for dy in OFFSETS]
SOURCES += [(2, dy) for dy in OFFSETS]


def attention_kernel(block_ref, query_ref, *refs):
    piece_refs, (out_ref, key_ref, vt_ref), score_refs = refs[:10], refs[10:13], refs[13:]
    block = block_ref[0]
    rows = query_ref.shape[0]
    seq = key_ref.shape[0]
    width = 2 * rows
    factor = math.log2(math.e) / math.sqrt(DH)

    @pl.when(pl.program_id(1) == 0)
    def _():
        start = 0
        for keys, values in zip(piece_refs[:5], piece_refs[5:]):
            stop = start + keys.shape[0]
            key_ref[start:stop, :] = keys[...]
            vt_ref[:, start:stop] = values[...].T
            start = stop

    row_less_key = lax.rem(
        lax.broadcasted_iota(jnp.int32, (rows, width), 1), jnp.int32(rows)
    ) - lax.broadcasted_iota(jnp.int32, (rows, width), 0)
    place_x, place_y = block // RING, lax.rem(block, RING)
    least = []
    for dx, dy in SOURCES:
        source_x = lax.rem(place_x + (dx + RING), RING)
        source_y = lax.rem(place_y + (dy + RING), RING)
        least.append((source_x * RING + source_y - block) * rows)

    def scores(pair):
        first = query_ref[:, 2 * pair * DH : (2 * pair + 1) * DH]
        second = query_ref[:, (2 * pair + 1) * DH : (2 * pair + 2) * DH]
        query_t = jnp.concatenate([first.T, second.T], axis=1)
        tops = []
        for chunk in range(seq // CHUNK):
            raw = dot(key_ref[chunk * CHUNK : (chunk + 1) * CHUNK, :], query_t)
            for sub in range(CHUNK // rows):
                at = chunk * CHUNK + sub * rows
                seen = jnp.where(
                    row_less_key >= least[at // rows], raw[sub * rows : (sub + 1) * rows], -jnp.inf
                )
                score_refs[pair][at : at + rows, :] = seen
                tops.append(jnp.max(seen, axis=0, keepdims=True))
        return functools.reduce(jnp.maximum, tops)

    def weigh(pair, top):
        total, weighted = 0.0, 0.0
        for chunk in range(seq // CHUNK):
            at = slice(chunk * CHUNK, (chunk + 1) * CHUNK)
            prob = jnp.exp2((score_refs[pair][at, :] - top) * factor)
            weighted = weighted + dot(vt_ref[:, at], prob.astype(BF16))
            total = total + jnp.sum(prob, axis=0, keepdims=True)
        result = weighted / total
        for head in range(2):
            out_ref[:, (2 * pair + head) * DH : (2 * pair + head + 1) * DH] = (
                result[:, head * rows : (head + 1) * rows].T.astype(BF16)
            )

    top = scores(0)
    for pair in range(1, PAIRS):
        next_top = scores(pair)
        weigh(pair - 1, top)
        top = next_top
    weigh(PAIRS - 1, top)


def attention(block, queries, pieces):
    rows = queries.shape[0]
    seq = sum(p.shape[0] for p in pieces)
    steps = HQ // KVH // 2 // PAIRS
    span = 2 * PAIRS * DH
    return pl.pallas_call(
        attention_kernel,
        out_shape=jax.ShapeDtypeStruct(queries.shape, BF16),
        grid_spec=pltpu.PrefetchScalarGridSpec(
            num_scalar_prefetch=1,
            grid=(KVH, steps),
            in_specs=[pl.BlockSpec((rows, span), lambda g, p, b: (0, g * steps + p))]
            + [pl.BlockSpec((x.shape[0], DH), lambda g, p, b: (0, g)) for x in pieces]
            + [pl.BlockSpec((x.shape[0], DH), lambda g, p, b: (0, KVH + g)) for x in pieces],
            out_specs=pl.BlockSpec((rows, span), lambda g, p, b: (0, g * steps + p)),
            scratch_shapes=[pltpu.VMEM((seq, DH), BF16), pltpu.VMEM((DH, seq), BF16)]
            + [pltpu.VMEM((seq, 2 * rows), F32)] * PAIRS,
        ),
        compiler_params=pltpu.CompilerParams(
            dimension_semantics=("arbitrary", "arbitrary"), vmem_limit_bytes=24 << 20
        ),
        cost_estimate=pl.CostEstimate(
            flops=4 * rows * seq * HQ * DH,
            bytes_accessed=4 * queries.size + 4 * seq * KVH * DH,
            transcendentals=rows * seq * HQ,
        ),
        name="attention",
    )(block, queries, *pieces, *pieces)


def shift_x(rows, step):
    pairs = [
        (x * RING + y, (x + step) % RING * RING + y) for x in range(RING) for y in range(RING)
    ]
    return lax.ppermute(rows, "ctx", pairs)


def shift_y(rows, step):
    pairs = [
        (x * RING + y, x * RING + (y + step) % RING) for x in range(RING) for y in range(RING)
    ]
    return lax.ppermute(rows, "ctx", pairs)


def gather_far(rows, shift):
    half = rows.shape[0] // 2
    before, after = shift(rows, 1), shift(rows, -1)
    return [rows, before, after, shift(before[:half], 1), shift(after[half:], -1)]


def gather_near(rows, shift):
    return jnp.concatenate([rows, shift(rows, 1), shift(rows, -1), shift(rows, 2)], axis=0)


def per_device(
    queries, keys, values, hidden, expert_ids, gate_probs, norm_gain, w_gate, w_up, w_down
):
    experts = lax.axis_size("ep")

    def exchange(rows):
        moved = lax.all_to_all(
            rows.reshape(experts, WHOLE, rows.shape[1]), "ep", split_axis=0, concat_axis=0, tiled=True
        )
        return moved.reshape(rows.shape)

    outgoing, place = dispatch(hidden[0], expert_ids[0].T, norm_gain[None], experts)
    outgoing, *shards = lax.optimization_barrier((outgoing, w_gate, w_up, w_down))
    received = exchange(outgoing)
    shards = jnp.concatenate([shard[0] for shard in shards], axis=1)
    half = shards.shape[0] // 2
    pieces = gather_far(gather_near(shards[:half], shift_y), shift_x)
    pieces += gather_far(gather_near(shards[half:], shift_x), shift_y)
    produced = expert(received, pieces)

    produced, keys, values = lax.optimization_barrier((produced, keys, values))
    returned = exchange(produced)
    keys_values = jnp.concatenate([keys[0], values[0]], axis=1)
    pieces = gather_far(gather_near(keys_values, shift_y), shift_x)
    block = lax.axis_index("ctx").astype(jnp.int32)[None]
    attended = attention(block, queries[0], pieces)
    mixed = combine(returned, place, gate_probs[0].T)
    return (attended[None], mixed[None])


def solution(mesh):
    split = P("ep", "ctx", None)
    return jax.shard_map(
        per_device,
        mesh=mesh,
        in_specs=(split,) * 6 + (P(),) + (split,) * 3,
        out_specs=(split, split),
        check_vma=False,
    )
```

```python
import functools
import math

import jax
import jax.numpy as jnp
from jax import lax
from jax.experimental import pallas as pl
from jax.experimental.pallas import tpu as pltpu
from jax.sharding import PartitionSpec as P

HQ = 32
KVH = 2
DH = 128
CAP = 12
WHOLE = 8
CHUNK = 512
RING = 4
HIDDEN_STEP = 256
PAIRS = 4
VMEM = 16 << 20
EXPERT_VMEM = 24
BF16 = jnp.bfloat16
F32 = jnp.float32


def dot(a, b):
    return jnp.dot(a, b, preferred_element_type=F32)


def dot_nt(a, b):
    return lax.dot_general(a, b, (((1,), (1,)), ((), ())), preferred_element_type=F32)


def dispatch_kernel(hidden_hbm, ids_hbm, gain_hbm, out_ref, place_ref, *scratch):
    hidden_ref, ids_ref, gain_ref, sems = scratch
    copies = [
        pltpu.make_async_copy(source, place, sems.at[index])
        for index, (source, place) in enumerate(
            ((ids_hbm, ids_ref), (hidden_hbm, hidden_ref), (gain_hbm, gain_ref))
        )
    ]
    for copy in copies:
        copy.start()
    rows, width = hidden_ref.shape
    half = width // 2
    experts = out_ref.shape[0] // WHOLE

    copies[0].wait()
    ids = ids_ref[...]
    first, second = ids[0:1, :], ids[1:2, :]
    expert_iota = lax.broadcasted_iota(jnp.int32, (experts, rows), 0)
    hot = [(expert_iota == ids_row).astype(F32) for ids_row in (first, second)]
    earlier = (
        lax.broadcasted_iota(jnp.int32, (rows, rows), 0)
        < lax.broadcasted_iota(jnp.int32, (rows, rows), 1)
    ).astype(BF16)
    before = [dot(h.astype(BF16), earlier) for h in hot]
    before[1] = before[1] + jnp.sum(hot[0], axis=1, keepdims=True)
    slots = [
        jnp.sum(h * b, axis=0, keepdims=True).astype(jnp.int32) for h, b in zip(hot, before)
    ]
    whole = [
        jnp.where(s < WHOLE, e * WHOLE + s, -1) for e, s in zip((first, second), slots)
    ]
    halves = [
        jnp.where(s < WHOLE, -2, e * WHOLE + 2 * (s - WHOLE))
        for e, s in zip((first, second), slots)
    ]
    slot_iota = lax.broadcasted_iota(jnp.int32, (experts * WHOLE, rows), 0)

    def onehot(targets):
        return ((slot_iota == targets[0]) | (slot_iota == targets[1])).astype(F32).astype(BF16)

    copies[1].wait()
    copies[2].wait()
    tokens = hidden_ref[...].astype(F32)
    mean_square = jnp.mean(tokens * tokens, axis=-1, keepdims=True)
    normed = (tokens * lax.rsqrt(mean_square + 1e-06) * gain_ref[...]).astype(BF16)
    out_ref[:, :width] = dot(onehot(whole), normed).astype(BF16)
    out_ref[:, width:] = (
        dot(onehot(halves), normed[:, :half])
        + dot(onehot([h + 1 for h in halves]), normed[:, half:])
    ).astype(BF16)
    place_ref[...] = jnp.concatenate(whole + halves + whole + halves, axis=0)


def dispatch(hidden, ids, gain, experts):
    rows, width = hidden.shape
    return pl.pallas_call(
        dispatch_kernel,
        out_shape=(
            jax.ShapeDtypeStruct((experts * WHOLE, width + width // 2), BF16),
            jax.ShapeDtypeStruct((8, rows), jnp.int32),
        ),
        in_specs=[pl.BlockSpec(memory_space=pltpu.HBM)] * 3,
        scratch_shapes=[
            pltpu.VMEM(hidden.shape, BF16),
            pltpu.VMEM(ids.shape, jnp.int32),
            pltpu.VMEM(gain.shape, F32),
            pltpu.SemaphoreType.DMA((3,)),
        ],
        compiler_params=pltpu.CompilerParams(vmem_limit_bytes=VMEM),
        name="dispatch",
    )(*[pltpu.with_memory_space_constraint(x, pltpu.HBM) for x in (hidden, ids, gain)])


def expert_kernel(rows_ref, *refs):
    *piece_refs, out_ref, x_ref, y_ref, act_ref, w_ref, sems = refs
    count = rows_ref.shape[0]
    width = x_ref.shape[1]
    half = width // 2
    hidden = act_ref.shape[1]
    steps = range(0, hidden, HIDDEN_STEP)

    waves = [[] for _ in range(len(steps) + 1)]
    base, used = 0, 0
    for ref in piece_refs:
        size = ref.shape[0]
        spans = [(max(s, base), min(s + HIDDEN_STEP, base + size), 0, 2 * width) for s in steps]
        spans.append((base, base + size, 2 * width, width))
        for wave, (low, high, lane, lanes) in zip(waves, spans):
            if low < high:
                source = ref.at[pl.ds(low - base, high - low), pl.ds(lane, lanes)]
                place = w_ref.at[pl.ds(low, high - low), pl.ds(lane, lanes)]
                wave.append(pltpu.make_async_copy(source, place, sems.at[used]))
                used += 1
        base += size

    def start(wave):
        for copy in waves[wave]:
            copy.start()

    def finish(wave):
        for copy in waves[wave]:
            copy.wait()

    start(0)
    start(1)
    extra = count // 2
    pick_row = lax.broadcasted_iota(jnp.int32, (extra, count), 0)
    pick_col = lax.broadcasted_iota(jnp.int32, (extra, count), 1)
    x_ref[pl.ds(0, count), :] = rows_ref[:, :width]
    tail = rows_ref[:, width:]
    for part in range(2):
        pick = (pick_col == 2 * pick_row + part).astype(F32).astype(BF16)
        x_ref[pl.ds(count, extra), pl.ds(part * half, half)] = dot(pick, tail).astype(BF16)

    for wave, low in enumerate(steps):
        finish(wave)
        if wave + 2 <= len(steps):
            start(wave + 2)
        at = slice(low, low + HIDDEN_STEP)
        x = x_ref[...]
        gate_pre = dot_nt(x, w_ref[at, :width])
        up_pre = dot_nt(x, w_ref[at, width : 2 * width])
        act_ref[:, at] = (gate_pre / (1.0 + jnp.exp(-gate_pre)) * up_pre).astype(BF16)
    finish(len(steps))
    act = act_ref[...]
    piece = width // 4
    for step in range(4):
        lanes = slice(step * piece, (step + 1) * piece)
        y = dot(act, w_ref[:, 2 * width + lanes.start : 2 * width + lanes.stop]).astype(BF16)
        out_ref[:, lanes] = y[:count]
        y_ref[:, lanes] = y[count:]
    put_row = lax.broadcasted_iota(jnp.int32, (count, extra), 0)
    put_col = lax.broadcasted_iota(jnp.int32, (count, extra), 1)
    total = 0.0
    for part in range(2):
        put = (put_row == 2 * put_col + part).astype(F32).astype(BF16)
        total = total + dot(put, y_ref[:, pl.ds(part * half, half)])
    out_ref[:, width:] = total.astype(BF16)


def expert(rows, pieces):
    count = rows.shape[0]
    hidden, width = sum(p.shape[0] for p in pieces), pieces[0].shape[1] // 3
    total = count // WHOLE * CAP
    return pl.pallas_call(
        expert_kernel,
        out_shape=jax.ShapeDtypeStruct(rows.shape, BF16),
        in_specs=[pl.BlockSpec(memory_space=pltpu.VMEM)]
        + [pl.BlockSpec(memory_space=pltpu.HBM)] * len(pieces),
        out_specs=pl.BlockSpec(memory_space=pltpu.VMEM),
        scratch_shapes=[
            pltpu.VMEM((total, width), BF16),
            pltpu.VMEM((total - count, width), BF16),
            pltpu.VMEM((total, hidden), BF16),
            pltpu.VMEM((hidden, 3 * width), BF16),
            pltpu.SemaphoreType.DMA((4 * len(pieces),)),
        ],
        compiler_params=pltpu.CompilerParams(vmem_limit_bytes=EXPERT_VMEM << 20),
        cost_estimate=pl.CostEstimate(
            flops=6 * total * hidden * width,
            bytes_accessed=6 * hidden * width + 4 * rows.size,
            transcendentals=total * hidden,
        ),
        name="expert",
    )(rows, *[pltpu.with_memory_space_constraint(piece, pltpu.HBM) for piece in pieces])


def combine_kernel(returned_ref, place_ref, prob_ref, out_ref):
    count = returned_ref.shape[0]
    rows, width = out_ref.shape
    half = width // 2
    place = place_ref[...].astype(F32).T.astype(jnp.int32)
    prob = prob_ref[...].T
    slot_iota = lax.broadcasted_iota(jnp.int32, (rows, count), 1)

    def onehot(column):
        return (slot_iota == column).astype(F32).astype(BF16)

    whole = [onehot(place[:, route : route + 1]) for route in range(2)]
    for part in range(2):
        lanes = pl.ds(part * half, half)
        mixture = 0.0
        for route in range(2):
            picked = dot(whole[route], returned_ref[:, lanes]) + dot(
                onehot(place[:, 2 + route : 3 + route] + part), returned_ref[:, width:]
            )
            mixture = mixture + prob[:, route : route + 1] * picked
        out_ref[:, lanes] = mixture.astype(BF16)


def combine(returned, place, prob):
    rows, width = place.shape[1], returned.shape[1] // 3 * 2
    return pl.pallas_call(
        combine_kernel,
        out_shape=jax.ShapeDtypeStruct((rows, width), BF16),
        compiler_params=pltpu.CompilerParams(vmem_limit_bytes=VMEM),
        name="combine",
    )(returned, place, prob)


OFFSETS = (0, -1, 1, 2)
SOURCES = [(dx, dy) for dx in (0, -1, 1) for dy in OFFSETS]
SOURCES += [(2, dy) for dy in OFFSETS]


def attention_kernel(block_ref, query_ref, *refs):
    piece_refs, (out_ref, key_ref, vt_ref), score_refs = refs[:10], refs[10:13], refs[13:]
    block = block_ref[0]
    rows = query_ref.shape[0]
    seq = key_ref.shape[0]
    width = 2 * rows
    factor = math.log2(math.e) / math.sqrt(DH)

    @pl.when(pl.program_id(1) == 0)
    def _():
        start = 0
        for keys, values in zip(piece_refs[:5], piece_refs[5:]):
            stop = start + keys.shape[0]
            key_ref[start:stop, :] = keys[...]
            vt_ref[:, start:stop] = values[...].T
            start = stop

    row_less_key = lax.rem(
        lax.broadcasted_iota(jnp.int32, (rows, width), 1), jnp.int32(rows)
    ) - lax.broadcasted_iota(jnp.int32, (rows, width), 0)
    place_x, place_y = block // RING, lax.rem(block, RING)
    least = []
    for dx, dy in SOURCES:
        source_x = lax.rem(place_x + (dx + RING), RING)
        source_y = lax.rem(place_y + (dy + RING), RING)
        least.append((source_x * RING + source_y - block) * rows)

    def scores(pair):
        first = query_ref[:, 2 * pair * DH : (2 * pair + 1) * DH]
        second = query_ref[:, (2 * pair + 1) * DH : (2 * pair + 2) * DH]
        query_t = jnp.concatenate([first.T, second.T], axis=1)
        tops = []
        for chunk in range(seq // CHUNK):
            raw = dot(key_ref[chunk * CHUNK : (chunk + 1) * CHUNK, :], query_t)
            for sub in range(CHUNK // rows):
                at = chunk * CHUNK + sub * rows
                seen = jnp.where(
                    row_less_key >= least[at // rows], raw[sub * rows : (sub + 1) * rows], -jnp.inf
                )
                score_refs[pair][at : at + rows, :] = seen
                tops.append(jnp.max(seen, axis=0, keepdims=True))
        return functools.reduce(jnp.maximum, tops)

    def weigh(pair, top):
        total, weighted = 0.0, 0.0
        for chunk in range(seq // CHUNK):
            at = slice(chunk * CHUNK, (chunk + 1) * CHUNK)
            prob = jnp.exp2((score_refs[pair][at, :] - top) * factor)
            weighted = weighted + dot(vt_ref[:, at], prob.astype(BF16))
            total = total + jnp.sum(prob, axis=0, keepdims=True)
        result = weighted / total
        for head in range(2):
            out_ref[:, (2 * pair + head) * DH : (2 * pair + head + 1) * DH] = (
                result[:, head * rows : (head + 1) * rows].T.astype(BF16)
            )

    top = scores(0)
    for pair in range(1, PAIRS):
        next_top = scores(pair)
        weigh(pair - 1, top)
        top = next_top
    weigh(PAIRS - 1, top)


def attention(block, queries, pieces):
    rows = queries.shape[0]
    seq = sum(p.shape[0] for p in pieces)
    steps = HQ // KVH // 2 // PAIRS
    span = 2 * PAIRS * DH
    return pl.pallas_call(
        attention_kernel,
        out_shape=jax.ShapeDtypeStruct(queries.shape, BF16),
        grid_spec=pltpu.PrefetchScalarGridSpec(
            num_scalar_prefetch=1,
            grid=(KVH, steps),
            in_specs=[pl.BlockSpec((rows, span), lambda g, p, b: (0, g * steps + p))]
            + [pl.BlockSpec((x.shape[0], DH), lambda g, p, b: (0, g)) for x in pieces]
            + [pl.BlockSpec((x.shape[0], DH), lambda g, p, b: (0, KVH + g)) for x in pieces],
            out_specs=pl.BlockSpec((rows, span), lambda g, p, b: (0, g * steps + p)),
            scratch_shapes=[pltpu.VMEM((seq, DH), BF16), pltpu.VMEM((DH, seq), BF16)]
            + [pltpu.VMEM((seq, 2 * rows), F32)] * PAIRS,
        ),
        compiler_params=pltpu.CompilerParams(
            dimension_semantics=("arbitrary", "arbitrary"), vmem_limit_bytes=24 << 20
        ),
        cost_estimate=pl.CostEstimate(
            flops=4 * rows * seq * HQ * DH,
            bytes_accessed=4 * queries.size + 4 * seq * KVH * DH,
            transcendentals=rows * seq * HQ,
        ),
        name="attention",
    )(block, queries, *pieces, *pieces)


def shift_x(rows, step):
    pairs = [
        (x * RING + y, (x + step) % RING * RING + y) for x in range(RING) for y in range(RING)
    ]
    return lax.ppermute(rows, "ctx", pairs)


def shift_y(rows, step):
    pairs = [
        (x * RING + y, x * RING + (y + step) % RING) for x in range(RING) for y in range(RING)
    ]
    return lax.ppermute(rows, "ctx", pairs)


def gather_far(rows, shift):
    half = rows.shape[0] // 2
    before, after = shift(rows, 1), shift(rows, -1)
    return [rows, before, after, shift(before[:half], 1), shift(after[half:], -1)]


def gather_near(rows, shift):
    return jnp.concatenate([rows, shift(rows, 1), shift(rows, -1), shift(rows, 2)], axis=0)


def shift_split(rows, phase, step):
    cores = lax.axis_size("ep")
    pairs = []
    for x in range(RING):
        for y in range(RING):
            for ep in range(cores):
                along_y = (phase + ep) % 2 == 0
                to_x = x if along_y else (x + step) % RING
                to_y = (y + step) % RING if along_y else y
                pairs.append(((x * RING + y) * cores + ep, (to_x * RING + to_y) * cores + ep))
    return lax.ppermute(rows, ("ctx", "ep"), pairs)


def gather_split(rows):
    before, after = shift_split(rows, 0, 1), shift_split(rows, 0, -1)
    top = jnp.concatenate([rows, before], axis=0)
    bottom = jnp.concatenate([after, shift_split(before, 0, 1)], axis=0)
    top_before, bottom_after = shift_split(top, 1, 1), shift_split(bottom, 1, -1)
    top_after, bottom_before = shift_split(top, 1, -1), shift_split(bottom, 1, 1)
    top_far, bottom_far = shift_split(top_before, 1, 1), shift_split(bottom_after, 1, -1)
    return [top, bottom, top_before, top_after, bottom_before, bottom_after, top_far, bottom_far]


def per_device(
    queries, keys, values, hidden, expert_ids, gate_probs, norm_gain, w_gate, w_up, w_down
):
    experts = lax.axis_size("ep")

    def exchange(rows):
        moved = lax.all_to_all(
            rows.reshape(experts, WHOLE, rows.shape[1]), "ep", split_axis=0, concat_axis=0, tiled=True
        )
        return moved.reshape(rows.shape)

    outgoing, place = dispatch(hidden[0], expert_ids[0].T, norm_gain[None], experts)
    outgoing, *shards = lax.optimization_barrier((outgoing, w_gate, w_up, w_down))
    received = exchange(outgoing)
    shards = jnp.concatenate([shard[0] for shard in shards], axis=1)
    produced = expert(received, gather_split(shards))

    produced, keys, values = lax.optimization_barrier((produced, keys, values))
    returned = exchange(produced)
    keys_values = jnp.concatenate([keys[0], values[0]], axis=1)
    pieces = gather_far(gather_near(keys_values, shift_y), shift_x)
    block = lax.axis_index("ctx").astype(jnp.int32)[None]
    attended = attention(block, queries[0], pieces)
    mixed = combine(returned, place, gate_probs[0].T)
    return (attended[None], mixed[None])


def solution(mesh):
    split = P("ep", "ctx", None)
    return jax.shard_map(
        per_device,
        mesh=mesh,
        in_specs=(split,) * 6 + (P(),) + (split,) * 3,
        out_specs=(split, split),
        check_vma=False,
    )
```

```python
import functools
import math

import jax
import jax.numpy as jnp
from jax import lax
from jax.experimental import pallas as pl
from jax.experimental.pallas import tpu as pltpu
from jax.sharding import PartitionSpec as P

HQ = 32
KVH = 2
DH = 128
CAP = 12
WHOLE = 8
CHUNK = 512
RING = 4
HIDDEN_STEP = 256
PAIRS = 4
VMEM = 16 << 20
EXPERT_VMEM = 24
BF16 = jnp.bfloat16
F32 = jnp.float32


def dot(a, b):
    return jnp.dot(a, b, preferred_element_type=F32)


def dot_nt(a, b):
    return lax.dot_general(a, b, (((1,), (1,)), ((), ())), preferred_element_type=F32)


def dispatch_kernel(hidden_hbm, ids_hbm, gain_hbm, out_ref, place_ref, *scratch):
    hidden_ref, ids_ref, gain_ref, sems = scratch
    copies = [
        pltpu.make_async_copy(source, place, sems.at[index])
        for index, (source, place) in enumerate(
            ((ids_hbm, ids_ref), (hidden_hbm, hidden_ref), (gain_hbm, gain_ref))
        )
    ]
    for copy in copies:
        copy.start()
    rows, width = hidden_ref.shape
    half = width // 2
    experts = out_ref.shape[0] // WHOLE

    copies[0].wait()
    ids = ids_ref[...]
    first, second = ids[0:1, :], ids[1:2, :]
    expert_iota = lax.broadcasted_iota(jnp.int32, (experts, rows), 0)
    hot = [(expert_iota == ids_row).astype(F32) for ids_row in (first, second)]
    earlier = (
        lax.broadcasted_iota(jnp.int32, (rows, rows), 0)
        < lax.broadcasted_iota(jnp.int32, (rows, rows), 1)
    ).astype(BF16)
    before = [dot(h.astype(BF16), earlier) for h in hot]
    before[1] = before[1] + jnp.sum(hot[0], axis=1, keepdims=True)
    slots = [
        jnp.sum(h * b, axis=0, keepdims=True).astype(jnp.int32) for h, b in zip(hot, before)
    ]
    whole = [
        jnp.where(s < WHOLE, e * WHOLE + s, -1) for e, s in zip((first, second), slots)
    ]
    halves = [
        jnp.where(s < WHOLE, -2, e * WHOLE + 2 * (s - WHOLE))
        for e, s in zip((first, second), slots)
    ]
    slot_iota = lax.broadcasted_iota(jnp.int32, (experts * WHOLE, rows), 0)

    def onehot(targets):
        return ((slot_iota == targets[0]) | (slot_iota == targets[1])).astype(F32).astype(BF16)

    copies[1].wait()
    copies[2].wait()
    tokens = hidden_ref[...].astype(F32)
    mean_square = jnp.mean(tokens * tokens, axis=-1, keepdims=True)
    normed = (tokens * lax.rsqrt(mean_square + 1e-06) * gain_ref[...]).astype(BF16)
    out_ref[:, :width] = dot(onehot(whole), normed).astype(BF16)
    out_ref[:, width:] = (
        dot(onehot(halves), normed[:, :half])
        + dot(onehot([h + 1 for h in halves]), normed[:, half:])
    ).astype(BF16)
    place_ref[...] = jnp.concatenate(whole + halves + whole + halves, axis=0)


def dispatch(hidden, ids, gain, experts):
    rows, width = hidden.shape
    return pl.pallas_call(
        dispatch_kernel,
        out_shape=(
            jax.ShapeDtypeStruct((experts * WHOLE, width + width // 2), BF16),
            jax.ShapeDtypeStruct((8, rows), jnp.int32),
        ),
        in_specs=[pl.BlockSpec(memory_space=pltpu.HBM)] * 3,
        scratch_shapes=[
            pltpu.VMEM(hidden.shape, BF16),
            pltpu.VMEM(ids.shape, jnp.int32),
            pltpu.VMEM(gain.shape, F32),
            pltpu.SemaphoreType.DMA((3,)),
        ],
        compiler_params=pltpu.CompilerParams(vmem_limit_bytes=VMEM),
        name="dispatch",
    )(*[pltpu.with_memory_space_constraint(x, pltpu.HBM) for x in (hidden, ids, gain)])


def expert_kernel(rows_ref, *refs):
    *piece_refs, out_ref, x_ref, y_ref, act_ref, w_ref, sems = refs
    count = rows_ref.shape[0]
    width = x_ref.shape[1]
    half = width // 2
    hidden = act_ref.shape[1]
    steps = range(0, hidden, HIDDEN_STEP)

    waves = [[] for _ in range(len(steps) + 1)]
    base, used = 0, 0
    for ref in piece_refs:
        size = ref.shape[0]
        spans = [(max(s, base), min(s + HIDDEN_STEP, base + size), 0, 2 * width) for s in steps]
        spans.append((base, base + size, 2 * width, width))
        for wave, (low, high, lane, lanes) in zip(waves, spans):
            if low < high:
                source = ref.at[pl.ds(low - base, high - low), pl.ds(lane, lanes)]
                place = w_ref.at[pl.ds(low, high - low), pl.ds(lane, lanes)]
                wave.append(pltpu.make_async_copy(source, place, sems.at[used]))
                used += 1
        base += size

    def start(wave):
        for copy in waves[wave]:
            copy.start()

    def finish(wave):
        for copy in waves[wave]:
            copy.wait()

    start(0)
    start(1)
    extra = count // 2
    pick_row = lax.broadcasted_iota(jnp.int32, (extra, count), 0)
    pick_col = lax.broadcasted_iota(jnp.int32, (extra, count), 1)
    x_ref[pl.ds(0, count), :] = rows_ref[:, :width]
    tail = rows_ref[:, width:]
    for part in range(2):
        pick = (pick_col == 2 * pick_row + part).astype(F32).astype(BF16)
        x_ref[pl.ds(count, extra), pl.ds(part * half, half)] = dot(pick, tail).astype(BF16)

    for wave, low in enumerate(steps):
        finish(wave)
        if wave + 2 <= len(steps):
            start(wave + 2)
        at = slice(low, low + HIDDEN_STEP)
        x = x_ref[...]
        gate_pre = dot_nt(x, w_ref[at, :width])
        up_pre = dot_nt(x, w_ref[at, width : 2 * width])
        act_ref[:, at] = (gate_pre / (1.0 + jnp.exp(-gate_pre)) * up_pre).astype(BF16)
    finish(len(steps))
    act = act_ref[...]
    piece = width // 4
    for step in range(4):
        lanes = slice(step * piece, (step + 1) * piece)
        y = dot(act, w_ref[:, 2 * width + lanes.start : 2 * width + lanes.stop]).astype(BF16)
        out_ref[:, lanes] = y[:count]
        y_ref[:, lanes] = y[count:]
    put_row = lax.broadcasted_iota(jnp.int32, (count, extra), 0)
    put_col = lax.broadcasted_iota(jnp.int32, (count, extra), 1)
    total = 0.0
    for part in range(2):
        put = (put_row == 2 * put_col + part).astype(F32).astype(BF16)
        total = total + dot(put, y_ref[:, pl.ds(part * half, half)])
    out_ref[:, width:] = total.astype(BF16)


def expert(rows, pieces):
    count = rows.shape[0]
    hidden, width = sum(p.shape[0] for p in pieces), pieces[0].shape[1] // 3
    total = count // WHOLE * CAP
    return pl.pallas_call(
        expert_kernel,
        out_shape=jax.ShapeDtypeStruct(rows.shape, BF16),
        in_specs=[pl.BlockSpec(memory_space=pltpu.VMEM)]
        + [pl.BlockSpec(memory_space=pltpu.HBM)] * len(pieces),
        out_specs=pl.BlockSpec(memory_space=pltpu.VMEM),
        scratch_shapes=[
            pltpu.VMEM((total, width), BF16),
            pltpu.VMEM((total - count, width), BF16),
            pltpu.VMEM((total, hidden), BF16),
            pltpu.VMEM((hidden, 3 * width), BF16),
            pltpu.SemaphoreType.DMA((4 * len(pieces),)),
        ],
        compiler_params=pltpu.CompilerParams(vmem_limit_bytes=EXPERT_VMEM << 20),
        cost_estimate=pl.CostEstimate(
            flops=6 * total * hidden * width,
            bytes_accessed=6 * hidden * width + 4 * rows.size,
            transcendentals=total * hidden,
        ),
        name="expert",
    )(rows, *[pltpu.with_memory_space_constraint(piece, pltpu.HBM) for piece in pieces])


def combine_kernel(returned_ref, place_ref, prob_ref, out_ref):
    count = returned_ref.shape[0]
    rows, width = out_ref.shape
    half = width // 2
    place = place_ref[...].astype(F32).T.astype(jnp.int32)
    prob = prob_ref[...].T
    slot_iota = lax.broadcasted_iota(jnp.int32, (rows, count), 1)

    def onehot(column):
        return (slot_iota == column).astype(F32).astype(BF16)

    whole = [onehot(place[:, route : route + 1]) for route in range(2)]
    for part in range(2):
        lanes = pl.ds(part * half, half)
        mixture = 0.0
        for route in range(2):
            picked = dot(whole[route], returned_ref[:, lanes]) + dot(
                onehot(place[:, 2 + route : 3 + route] + part), returned_ref[:, width:]
            )
            mixture = mixture + prob[:, route : route + 1] * picked
        out_ref[:, lanes] = mixture.astype(BF16)


def combine(returned, place, prob):
    rows, width = place.shape[1], returned.shape[1] // 3 * 2
    return pl.pallas_call(
        combine_kernel,
        out_shape=jax.ShapeDtypeStruct((rows, width), BF16),
        compiler_params=pltpu.CompilerParams(vmem_limit_bytes=VMEM),
        name="combine",
    )(returned, place, prob)


OFFSETS = (0, -1, 1, 2)
SOURCES = [(dx, dy) for dx in (0, -1, 1) for dy in OFFSETS]
SOURCES += [(2, dy) for dy in OFFSETS]


def attention_kernel(block_ref, query_ref, *refs):
    piece_refs, (out_ref, key_ref, vt_ref), score_refs = refs[:10], refs[10:13], refs[13:]
    block = block_ref[0]
    rows = query_ref.shape[0]
    seq = key_ref.shape[0]
    width = 2 * rows
    factor = math.log2(math.e) / math.sqrt(DH)

    @pl.when(pl.program_id(1) == 0)
    def _():
        start = 0
        for keys, values in zip(piece_refs[:5], piece_refs[5:]):
            stop = start + keys.shape[0]
            key_ref[start:stop, :] = keys[...]
            vt_ref[:, start:stop] = values[...].T
            start = stop

    row_less_key = lax.rem(
        lax.broadcasted_iota(jnp.int32, (rows, width), 1), jnp.int32(rows)
    ) - lax.broadcasted_iota(jnp.int32, (rows, width), 0)
    place_x, place_y = block // RING, lax.rem(block, RING)
    least = []
    for dx, dy in SOURCES:
        source_x = lax.rem(place_x + (dx + RING), RING)
        source_y = lax.rem(place_y + (dy + RING), RING)
        least.append((source_x * RING + source_y - block) * rows)

    def scores(pair):
        first = query_ref[:, 2 * pair * DH : (2 * pair + 1) * DH]
        second = query_ref[:, (2 * pair + 1) * DH : (2 * pair + 2) * DH]
        query_t = jnp.concatenate([first.T, second.T], axis=1)
        tops = []
        for chunk in range(seq // CHUNK):
            raw = dot(key_ref[chunk * CHUNK : (chunk + 1) * CHUNK, :], query_t)
            for sub in range(CHUNK // rows):
                at = chunk * CHUNK + sub * rows
                seen = jnp.where(
                    row_less_key >= least[at // rows], raw[sub * rows : (sub + 1) * rows], -jnp.inf
                )
                score_refs[pair][at : at + rows, :] = seen
                tops.append(jnp.max(seen, axis=0, keepdims=True))
        return functools.reduce(jnp.maximum, tops)

    def weigh(pair, top):
        total, weighted = 0.0, 0.0
        for chunk in range(seq // CHUNK):
            at = slice(chunk * CHUNK, (chunk + 1) * CHUNK)
            prob = jnp.exp2((score_refs[pair][at, :] - top) * factor)
            weighted = weighted + dot(vt_ref[:, at], prob.astype(BF16))
            total = total + jnp.sum(prob, axis=0, keepdims=True)
        result = weighted / total
        for head in range(2):
            out_ref[:, (2 * pair + head) * DH : (2 * pair + head + 1) * DH] = (
                result[:, head * rows : (head + 1) * rows].T.astype(BF16)
            )

    top = scores(0)
    for pair in range(1, PAIRS):
        next_top = scores(pair)
        weigh(pair - 1, top)
        top = next_top
    weigh(PAIRS - 1, top)


def attention(block, queries, pieces):
    rows = queries.shape[0]
    seq = sum(p.shape[0] for p in pieces)
    steps = HQ // KVH // 2 // PAIRS
    span = 2 * PAIRS * DH
    return pl.pallas_call(
        attention_kernel,
        out_shape=jax.ShapeDtypeStruct(queries.shape, BF16),
        grid_spec=pltpu.PrefetchScalarGridSpec(
            num_scalar_prefetch=1,
            grid=(KVH, steps),
            in_specs=[pl.BlockSpec((rows, span), lambda g, p, b: (0, g * steps + p))]
            + [pl.BlockSpec((x.shape[0], DH), lambda g, p, b: (0, g)) for x in pieces]
            + [pl.BlockSpec((x.shape[0], DH), lambda g, p, b: (0, KVH + g)) for x in pieces],
            out_specs=pl.BlockSpec((rows, span), lambda g, p, b: (0, g * steps + p)),
            scratch_shapes=[pltpu.VMEM((seq, DH), BF16), pltpu.VMEM((DH, seq), BF16)]
            + [pltpu.VMEM((seq, 2 * rows), F32)] * PAIRS,
        ),
        compiler_params=pltpu.CompilerParams(
            dimension_semantics=("arbitrary", "arbitrary"), vmem_limit_bytes=24 << 20
        ),
        cost_estimate=pl.CostEstimate(
            flops=4 * rows * seq * HQ * DH,
            bytes_accessed=4 * queries.size + 4 * seq * KVH * DH,
            transcendentals=rows * seq * HQ,
        ),
        name="attention",
    )(block, queries, *pieces, *pieces)


def shift_x(rows, step):
    pairs = [
        (x * RING + y, (x + step) % RING * RING + y) for x in range(RING) for y in range(RING)
    ]
    return lax.ppermute(rows, "ctx", pairs)


def shift_y(rows, step):
    pairs = [
        (x * RING + y, x * RING + (y + step) % RING) for x in range(RING) for y in range(RING)
    ]
    return lax.ppermute(rows, "ctx", pairs)


def gather_far(rows, shift):
    half = rows.shape[0] // 2
    before, after = shift(rows, 1), shift(rows, -1)
    return [rows, before, after, shift(before[:half], 1), shift(after[half:], -1)]


def gather_near(rows, shift):
    return jnp.concatenate([rows, shift(rows, 1), shift(rows, -1), shift(rows, 2)], axis=0)


def shift_split(rows, phase, step):
    cores = lax.axis_size("ep")
    pairs = []
    for x in range(RING):
        for y in range(RING):
            for ep in range(cores):
                along_y = (phase + ep) % 2 == 0
                to_x = x if along_y else (x + step) % RING
                to_y = (y + step) % RING if along_y else y
                pairs.append(((x * RING + y) * cores + ep, (to_x * RING + to_y) * cores + ep))
    return lax.ppermute(rows, ("ctx", "ep"), pairs)


def gather_blocks(own):
    def along(direction, rows, step):
        return shift_split(rows, direction, step)

    near = {
        (-1, 0): along(0, own, 1),
        (1, 0): along(0, own, -1),
        (0, -1): along(1, own, 1),
        (0, 1): along(1, own, -1),
    }
    corner = {
        (-1, -1): along(0, near[0, -1], 1),
        (1, 1): along(0, near[0, 1], -1),
        (1, -1): along(1, near[1, 0], 1),
        (-1, 1): along(1, near[-1, 0], -1),
    }
    far = {
        (2, 0): along(0, near[-1, 0], 1),
        (2, 1): along(0, corner[1, 1], -1),
        (0, 2): along(1, near[0, -1], 1),
        (1, 2): along(1, corner[1, 1], -1),
    }
    last = {
        (2, -1): along(0, corner[-1, -1], 1),
        (2, 2): along(0, far[1, 2], -1),
        (-1, 2): along(1, corner[-1, 1], -1),
    }
    return [own, *near.values(), *corner.values(), *far.values(), *last.values()]


def per_device(
    queries, keys, values, hidden, expert_ids, gate_probs, norm_gain, w_gate, w_up, w_down
):
    experts = lax.axis_size("ep")

    def exchange(rows):
        moved = lax.all_to_all(
            rows.reshape(experts, WHOLE, rows.shape[1]), "ep", split_axis=0, concat_axis=0, tiled=True
        )
        return moved.reshape(rows.shape)

    outgoing, place = dispatch(hidden[0], expert_ids[0].T, norm_gain[None], experts)
    outgoing, *shards = lax.optimization_barrier((outgoing, w_gate, w_up, w_down))
    received = exchange(outgoing)
    shards = jnp.concatenate([shard[0] for shard in shards], axis=1)
    produced = expert(received, gather_blocks(shards))

    produced, keys, values = lax.optimization_barrier((produced, keys, values))
    returned = exchange(produced)
    keys_values = jnp.concatenate([keys[0], values[0]], axis=1)
    pieces = gather_far(gather_near(keys_values, shift_y), shift_x)
    block = lax.axis_index("ctx").astype(jnp.int32)[None]
    attended = attention(block, queries[0], pieces)
    mixed = combine(returned, place, gate_probs[0].T)
    return (attended[None], mixed[None])


def solution(mesh):
    split = P("ep", "ctx", None)
    return jax.shard_map(
        per_device,
        mesh=mesh,
        in_specs=(split,) * 6 + (P(),) + (split,) * 3,
        out_specs=(split, split),
        check_vma=False,
    )
```

```python
import functools
import math

import jax
import jax.numpy as jnp
from jax import lax
from jax.experimental import pallas as pl
from jax.experimental.pallas import tpu as pltpu
from jax.sharding import PartitionSpec as P

HQ = 32
KVH = 2
DH = 128
CAP = 12
WHOLE = 8
CHUNK = 512
RING = 4
HIDDEN_STEP = 256
PAIRS = 4
VMEM = 16 << 20
EXPERT_VMEM = 24
BF16 = jnp.bfloat16
F32 = jnp.float32


def dot(a, b):
    return jnp.dot(a, b, preferred_element_type=F32)


def dot_nt(a, b):
    return lax.dot_general(a, b, (((1,), (1,)), ((), ())), preferred_element_type=F32)


def dispatch_kernel(hidden_hbm, ids_hbm, gain_hbm, out_ref, place_ref, *scratch):
    hidden_ref, ids_ref, gain_ref, sems = scratch
    copies = [
        pltpu.make_async_copy(source, place, sems.at[index])
        for index, (source, place) in enumerate(
            ((ids_hbm, ids_ref), (hidden_hbm, hidden_ref), (gain_hbm, gain_ref))
        )
    ]
    for copy in copies:
        copy.start()
    rows, width = hidden_ref.shape
    half = width // 2
    experts = out_ref.shape[0] // WHOLE

    copies[0].wait()
    ids = ids_ref[...]
    first, second = ids[0:1, :], ids[1:2, :]
    expert_iota = lax.broadcasted_iota(jnp.int32, (experts, rows), 0)
    hot = [(expert_iota == ids_row).astype(F32) for ids_row in (first, second)]
    earlier = (
        lax.broadcasted_iota(jnp.int32, (rows, rows), 0)
        < lax.broadcasted_iota(jnp.int32, (rows, rows), 1)
    ).astype(BF16)
    before = [dot(h.astype(BF16), earlier) for h in hot]
    before[1] = before[1] + jnp.sum(hot[0], axis=1, keepdims=True)
    slots = [
        jnp.sum(h * b, axis=0, keepdims=True).astype(jnp.int32) for h, b in zip(hot, before)
    ]
    whole = [
        jnp.where(s < WHOLE, e * WHOLE + s, -1) for e, s in zip((first, second), slots)
    ]
    halves = [
        jnp.where(s < WHOLE, -2, e * WHOLE + 2 * (s - WHOLE))
        for e, s in zip((first, second), slots)
    ]
    slot_iota = lax.broadcasted_iota(jnp.int32, (experts * WHOLE, rows), 0)

    def onehot(targets):
        return ((slot_iota == targets[0]) | (slot_iota == targets[1])).astype(F32).astype(BF16)

    copies[1].wait()
    copies[2].wait()
    tokens = hidden_ref[...].astype(F32)
    mean_square = jnp.mean(tokens * tokens, axis=-1, keepdims=True)
    normed = (tokens * lax.rsqrt(mean_square + 1e-06) * gain_ref[...]).astype(BF16)
    out_ref[:, :width] = dot(onehot(whole), normed).astype(BF16)
    out_ref[:, width:] = (
        dot(onehot(halves), normed[:, :half])
        + dot(onehot([h + 1 for h in halves]), normed[:, half:])
    ).astype(BF16)
    place_ref[...] = jnp.concatenate(whole + halves + whole + halves, axis=0)


def dispatch(hidden, ids, gain, experts):
    rows, width = hidden.shape
    return pl.pallas_call(
        dispatch_kernel,
        out_shape=(
            jax.ShapeDtypeStruct((experts * WHOLE, width + width // 2), BF16),
            jax.ShapeDtypeStruct((8, rows), jnp.int32),
        ),
        in_specs=[pl.BlockSpec(memory_space=pltpu.HBM)] * 3,
        scratch_shapes=[
            pltpu.VMEM(hidden.shape, BF16),
            pltpu.VMEM(ids.shape, jnp.int32),
            pltpu.VMEM(gain.shape, F32),
            pltpu.SemaphoreType.DMA((3,)),
        ],
        compiler_params=pltpu.CompilerParams(vmem_limit_bytes=VMEM),
        name="dispatch",
    )(*[pltpu.with_memory_space_constraint(x, pltpu.HBM) for x in (hidden, ids, gain)])


def expert_kernel(rows_ref, *refs):
    *piece_refs, out_ref, x_ref, y_ref, act_ref, w_ref, sems = refs
    count = rows_ref.shape[0]
    width = x_ref.shape[1]
    half = width // 2
    hidden = act_ref.shape[1]
    steps = range(0, hidden, HIDDEN_STEP)

    waves = [[] for _ in range(len(steps) + 1)]
    base, used = 0, 0
    for ref in piece_refs:
        size = ref.shape[0]
        spans = [(max(s, base), min(s + HIDDEN_STEP, base + size), 0, 2 * width) for s in steps]
        spans.append((base, base + size, 2 * width, width))
        for wave, (low, high, lane, lanes) in zip(waves, spans):
            if low < high:
                source = ref.at[pl.ds(low - base, high - low), pl.ds(lane, lanes)]
                place = w_ref.at[pl.ds(low, high - low), pl.ds(lane, lanes)]
                wave.append(pltpu.make_async_copy(source, place, sems.at[used]))
                used += 1
        base += size

    def start(wave):
        for copy in waves[wave]:
            copy.start()

    def finish(wave):
        for copy in waves[wave]:
            copy.wait()

    start(0)
    start(1)
    extra = count // 2
    pick_row = lax.broadcasted_iota(jnp.int32, (extra, count), 0)
    pick_col = lax.broadcasted_iota(jnp.int32, (extra, count), 1)
    x_ref[pl.ds(0, count), :] = rows_ref[:, :width]
    tail = rows_ref[:, width:]
    for part in range(2):
        pick = (pick_col == 2 * pick_row + part).astype(F32).astype(BF16)
        x_ref[pl.ds(count, extra), pl.ds(part * half, half)] = dot(pick, tail).astype(BF16)

    for wave, low in enumerate(steps):
        finish(wave)
        if wave + 2 <= len(steps):
            start(wave + 2)
        at = slice(low, low + HIDDEN_STEP)
        x = x_ref[...]
        gate_pre = dot_nt(x, w_ref[at, :width])
        up_pre = dot_nt(x, w_ref[at, width : 2 * width])
        act_ref[:, at] = (gate_pre / (1.0 + jnp.exp(-gate_pre)) * up_pre).astype(BF16)
    finish(len(steps))
    act = act_ref[...]
    piece = width // 4
    for step in range(4):
        lanes = slice(step * piece, (step + 1) * piece)
        y = dot(act, w_ref[:, 2 * width + lanes.start : 2 * width + lanes.stop]).astype(BF16)
        out_ref[:, lanes] = y[:count]
        y_ref[:, lanes] = y[count:]
    put_row = lax.broadcasted_iota(jnp.int32, (count, extra), 0)
    put_col = lax.broadcasted_iota(jnp.int32, (count, extra), 1)
    total = 0.0
    for part in range(2):
        put = (put_row == 2 * put_col + part).astype(F32).astype(BF16)
        total = total + dot(put, y_ref[:, pl.ds(part * half, half)])
    out_ref[:, width:] = total.astype(BF16)


def expert(rows, pieces):
    count = rows.shape[0]
    hidden, width = sum(p.shape[0] for p in pieces), pieces[0].shape[1] // 3
    total = count // WHOLE * CAP
    return pl.pallas_call(
        expert_kernel,
        out_shape=jax.ShapeDtypeStruct(rows.shape, BF16),
        in_specs=[pl.BlockSpec(memory_space=pltpu.VMEM)]
        + [pl.BlockSpec(memory_space=pltpu.HBM)] * len(pieces),
        out_specs=pl.BlockSpec(memory_space=pltpu.VMEM),
        scratch_shapes=[
            pltpu.VMEM((total, width), BF16),
            pltpu.VMEM((total - count, width), BF16),
            pltpu.VMEM((total, hidden), BF16),
            pltpu.VMEM((hidden, 3 * width), BF16),
            pltpu.SemaphoreType.DMA((4 * len(pieces),)),
        ],
        compiler_params=pltpu.CompilerParams(vmem_limit_bytes=EXPERT_VMEM << 20),
        cost_estimate=pl.CostEstimate(
            flops=6 * total * hidden * width,
            bytes_accessed=6 * hidden * width + 4 * rows.size,
            transcendentals=total * hidden,
        ),
        name="expert",
    )(rows, *[pltpu.with_memory_space_constraint(piece, pltpu.HBM) for piece in pieces])


def combine_kernel(returned_ref, place_ref, prob_ref, out_ref):
    count = returned_ref.shape[0]
    rows, width = out_ref.shape
    half = width // 2
    place = place_ref[...].astype(F32).T.astype(jnp.int32)
    prob = prob_ref[...].T
    slot_iota = lax.broadcasted_iota(jnp.int32, (rows, count), 1)

    def onehot(column):
        return (slot_iota == column).astype(F32).astype(BF16)

    whole = [onehot(place[:, route : route + 1]) for route in range(2)]
    for part in range(2):
        lanes = pl.ds(part * half, half)
        mixture = 0.0
        for route in range(2):
            picked = dot(whole[route], returned_ref[:, lanes]) + dot(
                onehot(place[:, 2 + route : 3 + route] + part), returned_ref[:, width:]
            )
            mixture = mixture + prob[:, route : route + 1] * picked
        out_ref[:, lanes] = mixture.astype(BF16)


def combine(returned, place, prob):
    rows, width = place.shape[1], returned.shape[1] // 3 * 2
    return pl.pallas_call(
        combine_kernel,
        out_shape=jax.ShapeDtypeStruct((rows, width), BF16),
        compiler_params=pltpu.CompilerParams(vmem_limit_bytes=VMEM),
        name="combine",
    )(returned, place, prob)


OFFSETS = (0, -1, 1, 2)
SOURCES = [(dx, dy) for dx in (0, -1, 1) for dy in OFFSETS]
SOURCES += [(2, dy) for dy in OFFSETS]


def attention_kernel(block_ref, query_ref, *refs):
    piece_refs, (out_ref, key_ref, vt_ref), score_refs = refs[:10], refs[10:13], refs[13:]
    block = block_ref[0]
    rows = query_ref.shape[0]
    seq = key_ref.shape[0]
    width = 2 * rows
    factor = math.log2(math.e) / math.sqrt(DH)

    @pl.when(pl.program_id(1) == 0)
    def _():
        start = 0
        for keys, values in zip(piece_refs[:5], piece_refs[5:]):
            stop = start + keys.shape[0]
            key_ref[start:stop, :] = keys[...]
            vt_ref[:, start:stop] = values[...].T
            start = stop

    row_less_key = lax.rem(
        lax.broadcasted_iota(jnp.int32, (rows, width), 1), jnp.int32(rows)
    ) - lax.broadcasted_iota(jnp.int32, (rows, width), 0)
    place_x, place_y = block // RING, lax.rem(block, RING)
    least = []
    for dx, dy in SOURCES:
        source_x = lax.rem(place_x + (dx + RING), RING)
        source_y = lax.rem(place_y + (dy + RING), RING)
        least.append((source_x * RING + source_y - block) * rows)

    def scores(pair):
        first = query_ref[:, 2 * pair * DH : (2 * pair + 1) * DH]
        second = query_ref[:, (2 * pair + 1) * DH : (2 * pair + 2) * DH]
        query_t = jnp.concatenate([first.T, second.T], axis=1)
        tops = []
        for chunk in range(seq // CHUNK):
            raw = dot(key_ref[chunk * CHUNK : (chunk + 1) * CHUNK, :], query_t)
            for sub in range(CHUNK // rows):
                at = chunk * CHUNK + sub * rows
                seen = jnp.where(
                    row_less_key >= least[at // rows], raw[sub * rows : (sub + 1) * rows], -jnp.inf
                )
                score_refs[pair][at : at + rows, :] = seen
                tops.append(jnp.max(seen, axis=0, keepdims=True))
        return functools.reduce(jnp.maximum, tops)

    def weigh(pair, top):
        total, weighted = 0.0, 0.0
        for chunk in range(seq // CHUNK):
            at = slice(chunk * CHUNK, (chunk + 1) * CHUNK)
            prob = jnp.exp2((score_refs[pair][at, :] - top) * factor)
            weighted = weighted + dot(vt_ref[:, at], prob.astype(BF16))
            total = total + jnp.sum(prob, axis=0, keepdims=True)
        result = weighted / total
        for head in range(2):
            out_ref[:, (2 * pair + head) * DH : (2 * pair + head + 1) * DH] = (
                result[:, head * rows : (head + 1) * rows].T.astype(BF16)
            )

    top = scores(0)
    for pair in range(1, PAIRS):
        next_top = scores(pair)
        weigh(pair - 1, top)
        top = next_top
    weigh(PAIRS - 1, top)


def attention(block, queries, pieces):
    rows = queries.shape[0]
    seq = sum(p.shape[0] for p in pieces)
    steps = HQ // KVH // 2 // PAIRS
    span = 2 * PAIRS * DH
    return pl.pallas_call(
        attention_kernel,
        out_shape=jax.ShapeDtypeStruct(queries.shape, BF16),
        grid_spec=pltpu.PrefetchScalarGridSpec(
            num_scalar_prefetch=1,
            grid=(KVH, steps),
            in_specs=[pl.BlockSpec((rows, span), lambda g, p, b: (0, g * steps + p))]
            + [pl.BlockSpec((x.shape[0], DH), lambda g, p, b: (0, g)) for x in pieces]
            + [pl.BlockSpec((x.shape[0], DH), lambda g, p, b: (0, KVH + g)) for x in pieces],
            out_specs=pl.BlockSpec((rows, span), lambda g, p, b: (0, g * steps + p)),
            scratch_shapes=[pltpu.VMEM((seq, DH), BF16), pltpu.VMEM((DH, seq), BF16)]
            + [pltpu.VMEM((seq, 2 * rows), F32)] * PAIRS,
        ),
        compiler_params=pltpu.CompilerParams(
            dimension_semantics=("arbitrary", "arbitrary"), vmem_limit_bytes=24 << 20
        ),
        cost_estimate=pl.CostEstimate(
            flops=4 * rows * seq * HQ * DH,
            bytes_accessed=4 * queries.size + 4 * seq * KVH * DH,
            transcendentals=rows * seq * HQ,
        ),
        name="attention",
    )(block, queries, *pieces, *pieces)


def shift_x(rows, step):
    pairs = [
        (x * RING + y, (x + step) % RING * RING + y) for x in range(RING) for y in range(RING)
    ]
    return lax.ppermute(rows, "ctx", pairs)


def shift_y(rows, step):
    pairs = [
        (x * RING + y, x * RING + (y + step) % RING) for x in range(RING) for y in range(RING)
    ]
    return lax.ppermute(rows, "ctx", pairs)


def gather_far(rows, shift):
    half = rows.shape[0] // 2
    before, after = shift(rows, 1), shift(rows, -1)
    return [rows, before, after, shift(before[:half], 1), shift(after[half:], -1)]


def gather_near(rows, shift):
    return jnp.concatenate([rows, shift(rows, 1), shift(rows, -1), shift(rows, 2)], axis=0)


def gather_blocks(own):
    def along(direction, rows, step):
        return (shift_x, shift_y)[direction](rows, step)

    near = {
        (-1, 0): along(0, own, 1),
        (1, 0): along(0, own, -1),
        (0, -1): along(1, own, 1),
        (0, 1): along(1, own, -1),
    }
    corner = {
        (-1, -1): along(0, near[0, -1], 1),
        (1, 1): along(0, near[0, 1], -1),
        (1, -1): along(1, near[1, 0], 1),
        (-1, 1): along(1, near[-1, 0], -1),
    }
    far = {
        (2, 0): along(0, near[-1, 0], 1),
        (2, 1): along(0, corner[1, 1], -1),
        (0, 2): along(1, near[0, -1], 1),
        (1, 2): along(1, corner[1, 1], -1),
    }
    last = {
        (2, -1): along(0, corner[-1, -1], 1),
        (2, 2): along(0, far[1, 2], -1),
        (-1, 2): along(1, corner[-1, 1], -1),
    }
    return [own, *near.values(), *corner.values(), *far.values(), *last.values()]


def per_device(
    queries, keys, values, hidden, expert_ids, gate_probs, norm_gain, w_gate, w_up, w_down
):
    experts = lax.axis_size("ep")

    def exchange(rows):
        moved = lax.all_to_all(
            rows.reshape(experts, WHOLE, rows.shape[1]), "ep", split_axis=0, concat_axis=0, tiled=True
        )
        return moved.reshape(rows.shape)

    outgoing, place = dispatch(hidden[0], expert_ids[0].T, norm_gain[None], experts)
    outgoing, *shards = lax.optimization_barrier((outgoing, w_gate, w_up, w_down))
    received = exchange(outgoing)
    shards = jnp.concatenate([shard[0] for shard in shards], axis=1)
    produced = expert(received, gather_blocks(shards))

    produced, keys, values = lax.optimization_barrier((produced, keys, values))
    returned = exchange(produced)
    keys_values = jnp.concatenate([keys[0], values[0]], axis=1)
    pieces = gather_far(gather_near(keys_values, shift_y), shift_x)
    block = lax.axis_index("ctx").astype(jnp.int32)[None]
    attended = attention(block, queries[0], pieces)
    mixed = combine(returned, place, gate_probs[0].T)
    return (attended[None], mixed[None])


def solution(mesh):
    split = P("ep", "ctx", None)
    return jax.shard_map(
        per_device,
        mesh=mesh,
        in_specs=(split,) * 6 + (P(),) + (split,) * 3,
        out_specs=(split, split),
        check_vma=False,
    )
```
